32 devices in a mesh: row: 4 (over z), col: 8 (over y, x, core).
Axes of the slice: x: 2, y: 2, z: 4, core: 2. Of those that a mesh axis runs over, the one named last changes fastest.
Arguments:
- pair_products: bfloat16 [32, 64, 64, 64], P(('row', 'col')), may hold values from -6 to 6
- pw_index: int32 [8192], replicated, may hold values from 4096 to 131071, as said below
- valence_band: int32 [32], replicated, may hold values from 0 to 2047
- conduction_band: int32 [32], replicated, may hold values from 0 to 2047
- valence_energy: float32 [2048], replicated, may hold values from -10 to -0.5
- conduction_energy: float32 [2048], replicated, may hold values from 0.5 to 10
- imag_freq: float32 [2], replicated, may hold values from 0.3 to 12
Outputs:
- chi0: float32 [2, 16384, 16384], P(None, 'row', 'col')
The draws below stay inside these ranges and needn't reach their ends.
Inputs may be any that keep to these rules, and one draw needn't show every extreme that they name: `pw_index`: distinct flat indices (first grid index slowest) of grid points whose first component lies in 1 to 31, so no G-vector is zero and none is the negative of another.
All inputs are finite; a program needn't handle non-finite values.
Results may differ from the reference program's by a relative error of at most 0.0048.
Values may be sent and summed in bfloat16 or wider, within the bound.
A program may use at most 128 MiB of HBM per device.

```python
import math
import jax
import jax.numpy as jnp
from jax import lax

GRID = 64
NG = 8192
NFREQ = 2
NV = 2048
NC = 2048
PAIRS = 32


def draw_pw_index(key, part):
    plane = GRID * GRID
    count = (GRID // 2 - 1) * plane
    scores = jax.random.permutation(key, count)
    scores = scores.at[0].set(count).at[count - 1].set(count + 1)
    chosen = lax.top_k(scores, NG)[1]
    return ((1 + chosen // plane) * plane + chosen % plane).astype(jnp.int32)


def set_ends(entries, key, low, high):
    longest = entries.shape.index(max(entries.shape))
    spots = []
    for shift in (0, 1):
        where = [jax.random.randint(jax.random.fold_in(key, axis), (), 0, length) for axis, length in enumerate(entries.shape)]
        where[longest] = (where[longest] + shift) % entries.shape[longest]
        spots.append(tuple(where))
    return entries.at[spots[0]].set(low).at[spots[1]].set(high)


def steps_of(own_key, dims, cuts, low, largest):
    def one(dim, blocks):
        heights = jax.random.uniform(jax.random.fold_in(jax.random.fold_in(own_key, 6), dim), (blocks,), jnp.float32, low / len(cuts), largest / len(cuts))
        return jnp.repeat(jnp.exp(heights), dims[dim] // blocks).reshape((-1,) + (1,) * (len(dims) - dim - 1))

    loudness = one(*cuts[0])
    for cut in cuts[1:]:
        loudness = loudness * one(*cut)
    return loudness


def normal_values(stream_key, extent, width, limit, cuts=(), held_as=jnp.bfloat16):
    drawn = jax.random.normal(stream_key, extent, jnp.float32) * width
    if len(cuts) > 0:
        drawn = steps_of(stream_key, extent, cuts, -0.22, 0.18) * drawn
    return jnp.clip(drawn, min=-limit, max=limit).astype(held_as)


def setup_inputs(seed: int = 0) -> dict:
    key_of = jax.random.split(jax.random.key(seed), 8)
    pair_products = normal_values(key_of[0], (PAIRS, GRID, GRID, GRID), 1.0, 6.0, ((0, 32),))
    pw_index = draw_pw_index(jax.random.fold_in(key_of[7], 71), 0)
    valence_band = set_ends(jax.random.randint(key_of[2], (PAIRS,), 0, NV), jax.random.fold_in(key_of[2], 1), 0, NV - 1).astype(jnp.int32)
    conduction_band = set_ends(jax.random.randint(key_of[3], (PAIRS,), 0, NC), jax.random.fold_in(key_of[3], 1), 0, NC - 1).astype(jnp.int32)
    valence_energy = jnp.clip(jax.random.uniform(key_of[4], (NV,), jnp.float32, -10.0, -0.5), -10.0, -0.5)
    conduction_energy = jnp.clip(jax.random.uniform(key_of[5], (NC,), jnp.float32, 0.5, 10.0), 0.5, 10.0)
    imag_freq = jnp.clip(jnp.exp(jax.random.uniform(key_of[6], (NFREQ,), jnp.float32, math.log(0.3), math.log(12.0))), 0.3, 12.0)
    return dict(pair_products=pair_products, pw_index=pw_index, valence_band=valence_band, conduction_band=conduction_band, valence_energy=valence_energy, conduction_energy=conduction_energy, imag_freq=imag_freq)


def pair_weights(valence_band, conduction_band, valence_energy, conduction_energy, imag_freq):
    gap = conduction_energy[conduction_band] - valence_energy[valence_band]
    total = valence_band.shape[0]
    return -4.0 * gap[:, None] / (gap[:, None] ** 2 + imag_freq[None, :] ** 2) / jnp.sqrt(jnp.float32(total))

def reference(pair_products, pw_index, valence_band, conduction_band, valence_energy, conduction_energy, imag_freq):
    scale = float(GRID) ** (-1.5)

    def single(product):
        spectrum = jnp.fft.fftn(product.astype(jnp.float32)).reshape(-1)
        picked = spectrum[pw_index]
        return (jnp.concatenate([jnp.real(picked), -jnp.imag(picked)]) * scale).astype(jnp.bfloat16)
    coefficients = lax.map(single, pair_products)
    weights = pair_weights(valence_band, conduction_band, valence_energy, conduction_energy, imag_freq)
    left = coefficients.astype(jnp.float32)
    results = []
    for freq in range(NFREQ):
        weighted = (left * weights[:, freq:freq + 1]).astype(jnp.bfloat16).astype(jnp.float32)
        results.append(jnp.dot(left.T, weighted, preferred_element_type=jnp.float32))
    return jnp.stack(results)
```

```python
import functools
import math

import jax
import jax.numpy as jnp
import numpy as np
from jax import lax
from jax.experimental import pallas as pl
from jax.experimental.pallas import tpu as pltpu
from jax.sharding import PartitionSpec as P

MESH = pl.DeviceIdType.MESH
LANES = 128


def split(values):
    high = values.astype(jnp.bfloat16)
    low = (values - high.astype(jnp.float32)).astype(jnp.bfloat16)
    return high, low


def fourier_tables(points):
    counter = np.arange(points)
    angles = (counter[:, None] * counter[None, :] % points) * (2.0 * math.pi / points)
    cosine, sine = np.cos(angles), np.sin(angles)
    along_z = np.concatenate([cosine, -sine, -sine, -cosine], axis=1)
    along_y = np.block([[cosine, sine], [-sine, cosine]])
    upper = points // 2
    along_x = np.concatenate([cosine[:upper], sine[:upper]], axis=1) * float(points) ** (-1.5)
    tables = []
    for table in (along_z, along_y, along_x):
        single = table.astype(np.float32)
        high = single.astype(jnp.bfloat16)
        low = (single - high.astype(np.float32)).astype(jnp.bfloat16)
        tables += [high, low]
    return tables


def dot(left, right):
    return lax.dot_general(
        left, right, (((1,), (0,)), ((), ())), preferred_element_type=jnp.float32
    )


def transform_kernel(
    x_ref, index_ref, zh_ref, zl_ref, yh_ref, yl_ref, xh_ref, xl_ref,
    by_row_ref, by_col_ref,
    first, second, spectrum, picked,
):
    points = x_ref.shape[0]
    upper = points // 2
    wide = 2 * points
    step = 8

    zh, zl = zh_ref[...], zl_ref[...]

    @pl.loop(0, points // step)
    def _(block):
        start = pl.multiple_of(block * step, step)
        data = x_ref[pl.ds(start, step)].reshape(step * points, points)
        rows = pl.ds(pl.multiple_of(start * points, step * points), step * points)
        first[rows, :] = dot(data, zh) + dot(data, zl)

    yh, yl = yh_ref[...], yl_ref[...]

    @pl.loop(0, points // 2, unroll=2)
    def _(pair):
        blocks = []
        for side in range(2):
            rows = pl.ds(pl.multiple_of((2 * pair + side) * points, points), points)
            blocks.append(jnp.concatenate([first[rows, :wide], first[rows, wide:]], axis=0))
        high, low = split(jnp.concatenate(blocks, axis=1))
        result = dot(yh, high) + (dot(yh, low) + dot(yl, high))
        for side in range(2):
            rows = pl.ds(pl.multiple_of((2 * pair + side) * wide, wide), wide)
            second[rows, :] = result[:, side * wide:(side + 1) * wide]

    xh, xl = xh_ref[...], xl_ref[...]
    per_group = spectrum.shape[1] // LANES
    groups = points // 2 // per_group
    half_rows = groups * upper
    lane = lax.broadcasted_iota(jnp.int32, (upper, wide), 1)

    for group in range(groups):

        @pl.loop(0, per_group, unroll=2)
        def _(place):
            base = 2 * (group * per_group + place)
            blocks = []
            for side in range(2):
                straight = second[pl.ds(base + side, points, stride=wide), :]
                turned = second[pl.ds(base + side + points, points, stride=wide), :]
                blocks.append(jnp.concatenate([straight, turned], axis=0))
            high, low = split(jnp.concatenate(blocks, axis=1))
            result = dot(xh, high) + (dot(xh, low) + dot(xl, high))
            even, odd = result[:, :wide], result[:, wide:]
            real = jnp.where(lane < points, even, pltpu.roll(odd, points, 1))
            imag = -jnp.where(lane < points, pltpu.roll(even, points, 1), odd)
            columns = pl.ds(pl.multiple_of(place * LANES, LANES), LANES)
            spectrum[group * upper:(group + 1) * upper, columns] = real.astype(jnp.bfloat16)
            spectrum[half_rows + group * upper:half_rows + (group + 1) * upper, columns] = (
                imag.astype(jnp.bfloat16)
            )

    depth = spectrum.shape[1]
    count = index_ref.shape[1]
    width = 256
    part = 256
    local = lax.broadcasted_iota(jnp.int32, (part, width), 0).astype(jnp.float32).astype(jnp.bfloat16)
    row_of = lax.broadcasted_iota(jnp.int32, (half_rows, width), 0)
    one = jnp.ones((part, width), jnp.bfloat16)
    zero = jnp.zeros((part, width), jnp.bfloat16)

    @pl.loop(0, count // width)
    def _(chunk):
        start = pl.multiple_of(chunk * width, width)
        index = index_ref[:, pl.ds(start, width)]
        column = index % depth
        upper_part = index // depth
        row = (upper_part % groups) * upper + upper_part // groups
        total = jnp.zeros((2 * half_rows, width), jnp.float32)
        for at in range(depth // part):
            shifted = (column - at * part).astype(jnp.float32).astype(jnp.bfloat16)
            chosen = jnp.where(local == jnp.broadcast_to(shifted, local.shape), one, zero)
            total = total + dot(spectrum[:, at * part:(at + 1) * part], chosen)
        mask = row_of == row
        real = jnp.sum(jnp.where(mask, total[:half_rows], 0.0), axis=0, keepdims=True)
        imag = jnp.sum(jnp.where(mask, total[half_rows:], 0.0), axis=0, keepdims=True)
        for side in range(width // LANES):
            line = chunk * (width // LANES) + side
            lanes = slice(side * LANES, (side + 1) * LANES)
            picked[pl.ds(line, 1), :] = real[:, lanes]
            picked[pl.ds(count // LANES + line, 1), :] = imag[:, lanes]

    for ref in (by_row_ref, by_col_ref):
        height = ref.shape[1]
        for block in range(ref.shape[0]):
            ref[block] = picked[block * height:(block + 1) * height, :].astype(jnp.bfloat16)


def transform(product, pw_index, row_count, col_count):
    points = product.shape[0]
    count = pw_index.shape[0]
    lines = 2 * count // LANES
    tables = [jnp.asarray(table) for table in fourier_tables(points)]
    depth = 1024
    whole = pl.BlockSpec(memory_space=pltpu.VMEM)
    return pl.pallas_call(
        transform_kernel,
        out_shape=(
            jax.ShapeDtypeStruct((row_count, lines // row_count, LANES), jnp.bfloat16),
            jax.ShapeDtypeStruct((col_count, lines // col_count, LANES), jnp.bfloat16),
        ),
        in_specs=[whole] * (2 + len(tables)),
        out_specs=(whole, whole),
        scratch_shapes=[
            pltpu.VMEM((points * points, 4 * points), jnp.float32),
            pltpu.VMEM((points * 2 * points, 2 * points), jnp.float32),
            pltpu.VMEM((points**3 // depth, depth), jnp.bfloat16),
            pltpu.VMEM((lines, LANES), jnp.float32),
        ],
        name="spectrum",
    )(product, pw_index.reshape(1, count), *tables)


def exchange_kernel(
    by_row, by_col, row_panel, col_panel,
    row_send, row_recv, col_send, col_recv,
    share_send, share_recv, pass_send, pass_recv, own_sem,
):
    rows, cols = row_panel.shape[:2]
    r, c = lax.axis_index("row"), lax.axis_index("col")

    barrier = pltpu.get_barrier_semaphore()

    def each(count, action):
        def body(step, carry):
            action(step)
            return carry

        lax.fori_loop(1, count, body, 0)

    each(rows, lambda i: pl.semaphore_signal(
        barrier, inc=1, device_id=(lax.rem(r + i, rows), c), device_id_type=MESH))
    each(cols, lambda k: pl.semaphore_signal(
        barrier, inc=1, device_id=(r, lax.rem(c + k, cols)), device_id_type=MESH))
    pl.semaphore_wait(barrier, rows + cols - 2)

    def remote(source, target, send, recv, device):
        return pltpu.make_async_remote_copy(
            src_ref=source, dst_ref=target, send_sem=send, recv_sem=recv,
            device_id=device, device_id_type=MESH)

    def row_copy(i, source):
        return remote(
            by_row.at[lax.rem(r + i, rows)], row_panel.at[source, c],
            row_send.at[i], row_recv.at[i], (lax.rem(r + i, rows), c))

    def col_copy(k, source):
        return remote(
            by_col.at[lax.rem(c + k, cols)], col_panel.at[r, source],
            col_send.at[k], col_recv.at[k], (r, lax.rem(c + k, cols)))

    def share(i, k, held, source):
        return remote(
            held, row_panel.at[lax.rem(r - i + rows, rows), source],
            share_send.at[i, k], share_recv.at[i, k], (r, lax.rem(c + k, cols)))

    def hand_on(i, source):
        return remote(
            col_panel.at[r], col_panel.at[source],
            pass_send.at[i], pass_recv.at[i], (lax.rem(r + i, rows), c))

    each(rows, lambda i: row_copy(i, r).start())
    each(cols, lambda k: col_copy(k, c).start())
    own_row = pltpu.make_async_copy(by_row.at[r], row_panel.at[r, c], own_sem.at[0])
    own_col = pltpu.make_async_copy(by_col.at[c], col_panel.at[r, c], own_sem.at[1])
    own_row.start()
    own_col.start()
    each(cols, lambda k: share(0, k, by_row.at[r], c).start())
    own_row.wait()
    own_col.wait()
    each(cols, lambda k: col_copy(k, lax.rem(c - k + cols, cols)).wait_recv())
    each(rows, lambda i: hand_on(i, r).start())

    def forward(i):
        source = lax.rem(r - i + rows, rows)
        row_copy(i, source).wait_recv()
        each(cols, lambda k: share(i, k, row_panel.at[source, c], c).start())

    each(rows, forward)

    def finish(i, carry):
        held = row_panel.at[lax.rem(r - i + rows, rows), c]

        def ending(k):
            share(i, k, held, lax.rem(c - k + cols, cols)).wait_recv()
            share(i, k, held, c).wait_send()

        each(cols, ending)
        return carry

    each(rows, lambda i: row_copy(i, r).wait_send())
    each(cols, lambda k: col_copy(k, c).wait_send())

    def passed(i):
        hand_on(i, lax.rem(r - i + rows, rows)).wait_recv()
        hand_on(i, r).wait_send()

    each(rows, passed)
    lax.fori_loop(0, rows, finish, 0)


def exchange(by_row, by_col):
    rows, cols = by_row.shape[0], by_col.shape[0]
    whole = pl.BlockSpec(memory_space=pltpu.VMEM)
    dma = pltpu.SemaphoreType.DMA
    return pl.pallas_call(
        exchange_kernel,
        out_shape=(
            jax.ShapeDtypeStruct((rows, cols) + by_row.shape[1:], jnp.bfloat16),
            jax.ShapeDtypeStruct((rows, cols) + by_col.shape[1:], jnp.bfloat16),
        ),
        in_specs=[whole, whole],
        out_specs=(whole, whole),
        scratch_shapes=[
            dma((rows,)), dma((rows,)), dma((cols,)), dma((cols,)),
            dma((rows, cols)), dma((rows, cols)), dma((rows,)), dma((rows,)), dma((2,)),
        ],
        compiler_params=pltpu.CompilerParams(collective_id=0, has_side_effects=True),
        name="exchange",
    )(by_row, by_col)


def product_kernel(row_ref, col_ref, weight_ref, out_ref, row_lines, col_lines, left, right):
    pairs = row_ref.shape[0]

    @pl.when(pl.program_id(0) == 0)
    def _():
        for ref, lines, is_left in ((row_ref, row_lines, True), (col_ref, col_lines, False)):
            if len(ref.shape) == 3:
                height = ref.shape[1]
                lines[...] = ref[...].astype(jnp.float32).reshape(lines.shape)
            else:
                height = ref.shape[1] // LANES
            for block in range(height):
                lanes = slice(block * LANES, (block + 1) * LANES)
                if len(ref.shape) == 3:
                    values = lines[pl.ds(block, pairs, stride=height), :]
                else:
                    values = ref[:, lanes].astype(jnp.float32)
                if is_left:
                    left[lanes, :] = values.T.astype(jnp.bfloat16)
                else:
                    for freq in range(out_ref.shape[0]):
                        right[freq, :, lanes] = (
                            values * weight_ref[:, freq:freq + 1]
                        ).astype(jnp.bfloat16)

    height = out_ref.shape[1]
    rows = pl.ds(pl.multiple_of(pl.program_id(0) * height, height), height)
    panel = left[rows, :]
    for freq in range(out_ref.shape[0]):
        out_ref[freq] = dot(panel, right[freq])


def product(row_panel, col_panel, weights):
    pairs, freq_count = weights.shape
    row_width = row_panel.shape[2] * LANES
    col_width = col_panel.shape[2] * LANES
    panels = []
    lines = []
    for panel in (row_panel, col_panel):
        height = panel.shape[2]
        if height % 16 == 0:
            panels.append(panel.reshape(pairs, height, LANES))
            lines.append(pltpu.VMEM((pairs * height, LANES), jnp.float32))
        else:
            panels.append(panel.reshape(pairs, height * LANES))
            lines.append(pltpu.VMEM((8, LANES), jnp.float32))
    block = min(256, row_width)
    whole = pl.BlockSpec(memory_space=pltpu.VMEM)
    return pl.pallas_call(
        product_kernel,
        grid=(row_width // block,),
        out_shape=jax.ShapeDtypeStruct((freq_count, row_width, col_width), jnp.float32),
        in_specs=[whole, whole, whole],
        out_specs=pl.BlockSpec((freq_count, block, col_width), lambda i: (0, i, 0)),
        scratch_shapes=lines + [
            pltpu.VMEM((row_width, pairs), jnp.bfloat16),
            pltpu.VMEM((freq_count, pairs, col_width), jnp.bfloat16),
        ],
        name="product",
    )(*panels, weights)


def lookup(indices, table):
    slots = jnp.arange(table.shape[0], dtype=jnp.int32)
    return jnp.sum(jnp.where(indices[:, None] == slots[None, :], table[None, :], 0.0), axis=1)


def pair_weights(valence_band, conduction_band, valence_energy, conduction_energy, imag_freq):
    gap = lookup(conduction_band, conduction_energy) - lookup(valence_band, valence_energy)
    total = valence_band.shape[0]
    return (
        -4.0
        * gap[:, None]
        / (gap[:, None] ** 2 + imag_freq[None, :] ** 2)
        / jnp.sqrt(jnp.float32(total))
    )


def shards(
    pair_products,
    pw_index,
    valence_band,
    conduction_band,
    valence_energy,
    conduction_energy,
    imag_freq,
):
    rows, cols = lax.axis_size("row"), lax.axis_size("col")
    by_row, by_col = transform(pair_products[0], pw_index, rows, cols)
    row_panel, col_panel = exchange(by_row, by_col)
    weights = pair_weights(
        valence_band, conduction_band, valence_energy, conduction_energy, imag_freq
    )
    return product(row_panel, col_panel, weights)


def solution(mesh):
    in_specs = (P(("row", "col"), None, None, None), P(), P(), P(), P(), P(), P())
    out_specs = P(None, "row", "col")
    return jax.shard_map(shards, mesh=mesh, in_specs=in_specs, out_specs=out_specs, check_vma=False)
```

```python
import functools
import math

import jax
import jax.numpy as jnp
import numpy as np
from jax import lax
from jax.experimental import pallas as pl
from jax.experimental.pallas import tpu as pltpu
from jax.sharding import PartitionSpec as P

MESH = pl.DeviceIdType.MESH
LANES = 128


def split(values):
    high = values.astype(jnp.bfloat16)
    low = (values - high.astype(jnp.float32)).astype(jnp.bfloat16)
    return high, low


def fourier_tables(points):
    counter = np.arange(points)
    angles = (counter[:, None] * counter[None, :] % points) * (2.0 * math.pi / points)
    cosine, sine = np.cos(angles), np.sin(angles)
    upper = points // 2

    def halves(table):
        single = table.astype(np.float32)
        high = single.astype(jnp.bfloat16)
        return high, (single - high.astype(np.float32)).astype(jnp.bfloat16)

    along_z = np.concatenate(halves(np.concatenate([cosine, -sine], axis=1)), axis=0)
    high, low = halves(np.concatenate([cosine, sine], axis=0))
    along_y = np.concatenate([high, high, low], axis=1)
    scale = float(points) ** (-1.5)
    high, low = halves(np.concatenate([cosine[:upper], sine[:upper]], axis=0) * scale)
    along_x = np.concatenate([high, high, low], axis=1)
    return [along_z, along_y, along_x]


def dot(left, right):
    return lax.dot_general(
        left, right, (((1,), (0,)), ((), ())), preferred_element_type=jnp.float32
    )


def transform_kernel(
    x_ref, index_ref, z_ref, y_ref, x_table_ref,
    by_row_ref, by_col_ref,
    planes, spectrum, picked,
):
    points = x_ref.shape[0]
    upper = points // 2
    wide = 2 * points
    step = 8
    along_z, along_y, along_x = z_ref[...], y_ref[...], x_table_ref[...]
    sign = jnp.where(lax.broadcasted_iota(jnp.int32, (points, wide), 1) < points, 1.0, -1.0)

    @pl.loop(0, points // step, unroll=2)
    def _(block):
        start = pl.multiple_of(block * step, step)
        data = x_ref[pl.ds(start, step)].reshape(step * points, points)
        lines = dot(jnp.concatenate([data, data], axis=1), along_z)
        high, low = split(lines)
        for pair in range(step // 2):
            blocks = []
            for side in range(2):
                rows = slice((2 * pair + side) * points, (2 * pair + side + 1) * points)
                blocks.append(jnp.concatenate([high[rows], low[rows], high[rows]], axis=0))
            result = dot(along_y, jnp.concatenate(blocks, axis=1))
            for side in range(2):
                part = result[:, side * wide:(side + 1) * wide]
                rows = pl.ds(pl.multiple_of((start + 2 * pair + side) * points, points), points)
                planes[rows, :] = part[:points] + sign * pltpu.roll(part[points:], points, 1)

    per_group = spectrum.shape[1] // LANES
    groups = points // 2 // per_group
    half_rows = groups * upper
    first_half = lax.broadcasted_iota(jnp.int32, (upper, wide), 1) < points

    for group in range(groups):

        @pl.loop(0, per_group, unroll=8)
        def _(place):
            base = 2 * (group * per_group + place)
            blocks = []
            for side in range(2):
                high, low = split(planes[pl.ds(base + side, points, stride=points), :])
                blocks.append(jnp.concatenate([high, low, high], axis=0))
            result = dot(along_x, jnp.concatenate(blocks, axis=1))
            even_cos, odd_cos = result[:upper, :wide], result[:upper, wide:]
            even_sin, odd_sin = result[upper:, :wide], result[upper:, wide:]

            def join(left, right, turn_left, turn_right):
                left = pltpu.roll(left, points, 1) if turn_left else left
                right = pltpu.roll(right, points, 1) if turn_right else right
                return jnp.where(first_half, left, right)

            real = join(even_cos, odd_cos, False, True) + join(even_sin, odd_sin, True, False)
            imag = join(even_sin, odd_sin, False, True) - join(even_cos, odd_cos, True, False)
            columns = pl.ds(pl.multiple_of(place * LANES, LANES), LANES)
            spectrum[group * upper:(group + 1) * upper, columns] = real.astype(jnp.bfloat16)
            spectrum[half_rows + group * upper:half_rows + (group + 1) * upper, columns] = (
                imag.astype(jnp.bfloat16)
            )

    depth = spectrum.shape[1]
    count = index_ref.shape[1]
    width = 256
    part = 256
    local = lax.broadcasted_iota(jnp.int32, (part, width), 0).astype(jnp.float32).astype(jnp.bfloat16)
    row_of = lax.broadcasted_iota(jnp.int32, (half_rows, width), 0)
    one = jnp.ones((part, width), jnp.bfloat16)
    zero = jnp.zeros((part, width), jnp.bfloat16)

    @pl.loop(0, count // width, unroll=8)
    def _(chunk):
        start = pl.multiple_of(chunk * width, width)
        index = index_ref[:, pl.ds(start, width)]
        column = index % depth
        upper_part = index // depth
        row = (upper_part % groups) * upper + upper_part // groups
        total = jnp.zeros((2 * half_rows, width), jnp.float32)
        for at in range(depth // part):
            shifted = (column - at * part).astype(jnp.float32).astype(jnp.bfloat16)
            chosen = jnp.where(local == jnp.broadcast_to(shifted, local.shape), one, zero)
            total = total + dot(spectrum[:, at * part:(at + 1) * part], chosen)
        mask = row_of == row
        real = jnp.sum(jnp.where(mask, total[:half_rows], 0.0), axis=0, keepdims=True)
        imag = jnp.sum(jnp.where(mask, total[half_rows:], 0.0), axis=0, keepdims=True)
        for side in range(width // LANES):
            line = chunk * (width // LANES) + side
            lanes = slice(side * LANES, (side + 1) * LANES)
            picked[pl.ds(line, 1), :] = real[:, lanes]
            picked[pl.ds(count // LANES + line, 1), :] = imag[:, lanes]

    for ref in (by_row_ref, by_col_ref):
        height = ref.shape[1]
        for block in range(ref.shape[0]):
            ref[block] = picked[block * height:(block + 1) * height, :].astype(jnp.bfloat16)


def transform(product, pw_index, row_count, col_count):
    points = product.shape[0]
    count = pw_index.shape[0]
    lines = 2 * count // LANES
    tables = [jnp.asarray(table) for table in fourier_tables(points)]
    depth = 1024
    whole = pl.BlockSpec(memory_space=pltpu.VMEM)
    return pl.pallas_call(
        transform_kernel,
        out_shape=(
            jax.ShapeDtypeStruct((row_count, lines // row_count, LANES), jnp.bfloat16),
            jax.ShapeDtypeStruct((col_count, lines // col_count, LANES), jnp.bfloat16),
        ),
        in_specs=[whole] * (2 + len(tables)),
        out_specs=(whole, whole),
        scratch_shapes=[
            pltpu.VMEM((points * points, 2 * points), jnp.float32),
            pltpu.VMEM((points**3 // depth, depth), jnp.bfloat16),
            pltpu.VMEM((lines, LANES), jnp.float32),
        ],
        name="spectrum",
    )(product, pw_index.reshape(1, count), *tables)


def column_of(row):
    size = row.shape[1]
    here = lax.broadcasted_iota(jnp.int32, (size, size), 0)
    there = lax.broadcasted_iota(jnp.int32, (size, size), 1)
    return jnp.sum(jnp.where(here == there, row, 0.0), axis=1, keepdims=True)


def lookup(indices, table):
    column = column_of(indices.astype(jnp.float32))
    slots = lax.broadcasted_iota(jnp.int32, (column.shape[0], table.shape[1]), 1)
    return jnp.sum(
        jnp.where(column == slots.astype(jnp.float32), table, 0.0), axis=1, keepdims=True
    )


def exchange_kernel(
    by_row, by_col, valence_band, conduction_band, valence_energy, conduction_energy, imag_freq,
    row_panel, col_panel, weights,
    row_send, row_recv, col_send, col_recv,
    share_send, share_recv, pass_send, pass_recv, own_sem,
):
    rows, cols = row_panel.shape[:2]
    r, c = lax.axis_index("row"), lax.axis_index("col")

    barrier = pltpu.get_barrier_semaphore()

    def each(count, action):
        def body(step, carry):
            action(step)
            return carry

        lax.fori_loop(1, count, body, 0)

    each(rows, lambda i: pl.semaphore_signal(
        barrier, inc=1, device_id=(lax.rem(r + i, rows), c), device_id_type=MESH))
    each(cols, lambda k: pl.semaphore_signal(
        barrier, inc=1, device_id=(r, lax.rem(c + k, cols)), device_id_type=MESH))
    pl.semaphore_wait(barrier, rows + cols - 2)

    def remote(source, target, send, recv, device):
        return pltpu.make_async_remote_copy(
            src_ref=source, dst_ref=target, send_sem=send, recv_sem=recv,
            device_id=device, device_id_type=MESH)

    def row_copy(i, source):
        return remote(
            by_row.at[lax.rem(r + i, rows)], row_panel.at[source, c],
            row_send.at[i], row_recv.at[i], (lax.rem(r + i, rows), c))

    def col_copy(k, source):
        return remote(
            by_col.at[lax.rem(c + k, cols)], col_panel.at[r, source],
            col_send.at[k], col_recv.at[k], (r, lax.rem(c + k, cols)))

    def share(i, k, held, source):
        return remote(
            held, row_panel.at[lax.rem(r - i + rows, rows), source],
            share_send.at[i, k], share_recv.at[i, k], (r, lax.rem(c + k, cols)))

    def hand_on(i, source):
        return remote(
            col_panel.at[r], col_panel.at[source],
            pass_send.at[i], pass_recv.at[i], (lax.rem(r + i, rows), c))

    each(rows, lambda i: row_copy(i, r).start())
    each(cols, lambda k: col_copy(k, c).start())
    own_row = pltpu.make_async_copy(by_row.at[r], row_panel.at[r, c], own_sem.at[0])
    own_col = pltpu.make_async_copy(by_col.at[c], col_panel.at[r, c], own_sem.at[1])
    own_row.start()
    own_col.start()
    each(cols, lambda k: share(0, k, by_row.at[r], c).start())
    gap = lookup(conduction_band[...], conduction_energy[...]) - lookup(
        valence_band[...], valence_energy[...]
    )
    root = math.sqrt(gap.shape[0])
    for freq in range(weights.shape[1]):
        omega = imag_freq[:, freq:freq + 1]
        weights[:, freq:freq + 1] = -4.0 * gap / (gap * gap + omega * omega) / root
    own_row.wait()
    own_col.wait()
    each(cols, lambda k: col_copy(k, lax.rem(c - k + cols, cols)).wait_recv())
    each(rows, lambda i: hand_on(i, r).start())

    def forward(i):
        source = lax.rem(r - i + rows, rows)
        row_copy(i, source).wait_recv()
        each(cols, lambda k: share(i, k, row_panel.at[source, c], c).start())

    each(rows, forward)

    def finish(i, carry):
        held = row_panel.at[lax.rem(r - i + rows, rows), c]

        def ending(k):
            share(i, k, held, lax.rem(c - k + cols, cols)).wait_recv()
            share(i, k, held, c).wait_send()

        each(cols, ending)
        return carry

    each(rows, lambda i: row_copy(i, r).wait_send())
    each(cols, lambda k: col_copy(k, c).wait_send())

    def passed(i):
        hand_on(i, lax.rem(r - i + rows, rows)).wait_recv()
        hand_on(i, r).wait_send()

    each(rows, passed)
    lax.fori_loop(0, rows, finish, 0)


def exchange(by_row, by_col, *bands):
    bands = [values.reshape(1, -1) for values in bands]
    rows, cols = by_row.shape[0], by_col.shape[0]
    whole = pl.BlockSpec(memory_space=pltpu.VMEM)
    dma = pltpu.SemaphoreType.DMA
    return pl.pallas_call(
        exchange_kernel,
        out_shape=(
            jax.ShapeDtypeStruct((rows, cols) + by_row.shape[1:], jnp.bfloat16),
            jax.ShapeDtypeStruct((rows, cols) + by_col.shape[1:], jnp.bfloat16),
            jax.ShapeDtypeStruct((bands[0].shape[1], bands[-1].shape[1]), jnp.float32),
        ),
        in_specs=[whole] * (2 + len(bands)),
        out_specs=(whole, whole, whole),
        scratch_shapes=[
            dma((rows,)), dma((rows,)), dma((cols,)), dma((cols,)),
            dma((rows, cols)), dma((rows, cols)), dma((rows,)), dma((rows,)), dma((2,)),
        ],
        compiler_params=pltpu.CompilerParams(collective_id=0, has_side_effects=True),
        name="exchange",
    )(by_row, by_col, *bands)


def product_kernel(row_ref, col_ref, weight_ref, out_ref, row_lines, col_lines, left, right, ring, sems):
    pairs = row_ref.shape[0]
    freq_count, row_width, _ = out_ref.shape
    slots, height = ring.shape[0], ring.shape[1]

    for ref, lines, is_left in ((row_ref, row_lines, True), (col_ref, col_lines, False)):
        if len(ref.shape) == 3:
            blocks = ref.shape[1]
            lines[...] = ref[...].astype(jnp.float32).reshape(lines.shape)
        else:
            blocks = ref.shape[1] // LANES
        for block in range(blocks):
            lanes = slice(block * LANES, (block + 1) * LANES)
            if len(ref.shape) == 3:
                values = lines[pl.ds(block, pairs, stride=blocks), :]
            else:
                values = ref[:, lanes].astype(jnp.float32)
            if is_left:
                left[lanes, :] = values.T.astype(jnp.bfloat16)
            else:
                for freq in range(freq_count):
                    right[freq, :, lanes] = (
                        values * weight_ref[:, freq:freq + 1]
                    ).astype(jnp.bfloat16)

    steps = row_width // height

    def write(slot, freq, step):
        rows = pl.ds(pl.multiple_of(step * height, height), height)
        return pltpu.make_async_copy(ring.at[slot], out_ref.at[freq, rows], sems.at[slot])

    @pl.loop(0, steps)
    def _(step):
        panel = left[pl.ds(pl.multiple_of(step * height, height), height), :]
        for freq in range(freq_count):
            unit = step * freq_count + freq
            slot = lax.rem(unit, slots)

            @pl.when(unit >= slots)
            def _():
                write(slot, freq, step).wait()

            ring[slot] = dot(panel, right[freq])
            write(slot, freq, step).start()

    for slot in range(min(slots, steps * freq_count)):
        write(slot, 0, 0).wait()


def product(row_panel, col_panel, weights):
    pairs, freq_count = weights.shape
    row_width = row_panel.shape[2] * LANES
    col_width = col_panel.shape[2] * LANES
    panels = []
    lines = []
    for panel in (row_panel, col_panel):
        height = panel.shape[2]
        if height % 16 == 0:
            panels.append(panel.reshape(pairs, height, LANES))
            lines.append(pltpu.VMEM((pairs * height, LANES), jnp.float32))
        else:
            panels.append(panel.reshape(pairs, height * LANES))
            lines.append(pltpu.VMEM((8, LANES), jnp.float32))
    block = min(256, row_width)
    slots = 4
    whole = pl.BlockSpec(memory_space=pltpu.VMEM)
    return pl.pallas_call(
        product_kernel,
        out_shape=jax.ShapeDtypeStruct((freq_count, row_width, col_width), jnp.float32),
        in_specs=[whole, whole, whole],
        out_specs=pl.BlockSpec(memory_space=pl.ANY),
        scratch_shapes=lines + [
            pltpu.VMEM((row_width, pairs), jnp.bfloat16),
            pltpu.VMEM((freq_count, pairs, col_width), jnp.bfloat16),
            pltpu.VMEM((slots, block, col_width), jnp.float32),
            pltpu.SemaphoreType.DMA((slots,)),
        ],
        name="product",
    )(*panels, weights)


def shards(
    pair_products,
    pw_index,
    valence_band,
    conduction_band,
    valence_energy,
    conduction_energy,
    imag_freq,
):
    rows, cols = lax.axis_size("row"), lax.axis_size("col")
    by_row, by_col = transform(pair_products[0], pw_index, rows, cols)
    row_panel, col_panel, weights = exchange(
        by_row, by_col,
        valence_band, conduction_band, valence_energy, conduction_energy, imag_freq,
    )
    return product(row_panel, col_panel, weights)


def solution(mesh):
    in_specs = (P(("row", "col"), None, None, None), P(), P(), P(), P(), P(), P())
    out_specs = P(None, "row", "col")
    return jax.shard_map(shards, mesh=mesh, in_specs=in_specs, out_specs=out_specs, check_vma=False)
```

```python
import math

import jax
import jax.numpy as jnp
import numpy as np
from jax import lax
from jax.experimental import pallas as pl
from jax.experimental.pallas import tpu as pltpu
from jax.sharding import PartitionSpec as P

MESH = pl.DeviceIdType.MESH
LANES = 128


def split(values):
    high = values.astype(jnp.bfloat16)
    low = (values - high.astype(jnp.float32)).astype(jnp.bfloat16)
    return high, low


def fourier_tables(points):
    counter = np.arange(points)
    angles = (counter[:, None] * counter[None, :] % points) * (2.0 * math.pi / points)
    cosine, sine = np.cos(angles), np.sin(angles)
    upper = points // 2

    def halves(table):
        single = table.astype(np.float32)
        high = single.astype(jnp.bfloat16)
        return high, (single - high.astype(np.float32)).astype(jnp.bfloat16)

    along_z = np.concatenate(halves(np.concatenate([cosine, -sine], axis=1)), axis=0)
    high, low = halves(np.concatenate([cosine, sine], axis=0))
    along_y = np.concatenate([high, high, low], axis=1)
    scale = float(points) ** (-1.5)
    high, low = halves(np.concatenate([cosine[:upper], sine[:upper]], axis=0) * scale)
    along_x = np.concatenate([high, high, low], axis=1)
    return [along_z, along_y, along_x]


def dot(left, right):
    return lax.dot_general(
        left, right, (((1,), (0,)), ((), ())), preferred_element_type=jnp.float32
    )


def column_of(row):
    size = row.shape[1]
    here = lax.broadcasted_iota(jnp.int32, (size, size), 0)
    there = lax.broadcasted_iota(jnp.int32, (size, size), 1)
    return jnp.sum(jnp.where(here == there, row, 0.0), axis=1, keepdims=True)


def lookup(indices, table):
    column = column_of(indices.astype(jnp.float32))
    slots = lax.broadcasted_iota(jnp.int32, (column.shape[0], table.shape[1]), 1)
    return jnp.sum(
        jnp.where(column == slots.astype(jnp.float32), table, 0.0), axis=1, keepdims=True
    )


def transform_kernel(
    x_ref, index_ref, z_ref, y_ref, x_table_ref,
    valence_band, conduction_band, valence_energy, conduction_energy, imag_freq,
    row_panel, col_panel, weights,
    planes, spectrum, picked, by_row, by_col,
    row_send, row_recv, col_send, col_recv,
    share_send, share_recv, pass_send, pass_recv,
):
    rows, cols, tall = row_panel.shape[:3]
    short = col_panel.shape[2]
    phases = row_send.shape[0]
    chunk_lines = tall // phases
    r, c = lax.axis_index("row"), lax.axis_index("col")

    def each(count, action):
        def body(step, carry):
            action(step)
            return carry

        lax.fori_loop(1, count, body, 0)

    def ahead(i):
        return lax.rem(r + i, rows)

    def behind(i):
        return lax.rem(r - i + rows, rows)

    def onward(k):
        return lax.rem(c + k, cols)

    def back(k):
        return lax.rem(c - k + cols, cols)

    def remote(source, target, send, recv, device):
        return pltpu.make_async_remote_copy(
            src_ref=source, dst_ref=target, send_sem=send, recv_sem=recv,
            device_id=device, device_id_type=MESH)

    def lines_of(phase):
        return pl.ds(phase * chunk_lines, chunk_lines)

    def row_copy(phase, i, source):
        return remote(
            by_row.at[ahead(i), lines_of(phase)], row_panel.at[source, c, lines_of(phase)],
            row_send.at[phase, i], row_recv.at[phase, i], (ahead(i), c))

    def col_copy(k, source):
        return remote(
            by_col.at[onward(k)], col_panel.at[r, source],
            col_send.at[k], col_recv.at[k], (r, onward(k)))

    def share(phase, i, k, held, source):
        return remote(
            held, row_panel.at[behind(i), source, lines_of(phase)],
            share_send.at[phase, i, k], share_recv.at[phase, i, k], (r, onward(k)))

    def hand_on(i, source):
        return remote(
            col_panel.at[r], col_panel.at[source],
            pass_send.at[i], pass_recv.at[i], (ahead(i), c))

    barrier = pltpu.get_barrier_semaphore()
    each(rows, lambda i: pl.semaphore_signal(
        barrier, inc=1, device_id=(ahead(i), c), device_id_type=MESH))
    each(cols, lambda k: pl.semaphore_signal(
        barrier, inc=1, device_id=(r, onward(k)), device_id_type=MESH))

    points = x_ref.shape[0]
    upper = points // 2
    wide = 2 * points
    step = 8
    along_z, along_y, along_x = z_ref[...], y_ref[...], x_table_ref[...]
    sign = jnp.where(lax.broadcasted_iota(jnp.int32, (points, wide), 1) < points, 1.0, -1.0)

    @pl.loop(0, points // step, unroll=2)
    def _(block):
        start = pl.multiple_of(block * step, step)
        data = x_ref[pl.ds(start, step)].reshape(step * points, points)
        lines = dot(jnp.concatenate([data, data], axis=1), along_z)
        high, low = split(lines)
        for pair in range(step // 2):
            blocks = []
            for side in range(2):
                rows = slice((2 * pair + side) * points, (2 * pair + side + 1) * points)
                blocks.append(jnp.concatenate([high[rows], low[rows], high[rows]], axis=0))
            result = dot(along_y, jnp.concatenate(blocks, axis=1))
            for side in range(2):
                part = result[:, side * wide:(side + 1) * wide]
                rows = pl.ds(pl.multiple_of((start + 2 * pair + side) * points, points), points)
                planes[rows, :] = part[:points] + sign * pltpu.roll(part[points:], points, 1)

    per_group = spectrum.shape[1] // LANES
    groups = points // 2 // per_group
    half_rows = groups * upper
    first_half = lax.broadcasted_iota(jnp.int32, (upper, wide), 1) < points

    for group in range(groups):

        @pl.loop(0, per_group, unroll=8)
        def _(place):
            base = 2 * (group * per_group + place)
            blocks = []
            for side in range(2):
                high, low = split(planes[pl.ds(base + side, points, stride=points), :])
                blocks.append(jnp.concatenate([high, low, high], axis=0))
            result = dot(along_x, jnp.concatenate(blocks, axis=1))
            even_cos, odd_cos = result[:upper, :wide], result[:upper, wide:]
            even_sin, odd_sin = result[upper:, :wide], result[upper:, wide:]

            def join(left, right, turn_left, turn_right):
                left = pltpu.roll(left, points, 1) if turn_left else left
                right = pltpu.roll(right, points, 1) if turn_right else right
                return jnp.where(first_half, left, right)

            real = join(even_cos, odd_cos, False, True) + join(even_sin, odd_sin, True, False)
            imag = join(even_sin, odd_sin, False, True) - join(even_cos, odd_cos, True, False)
            columns = pl.ds(pl.multiple_of(place * LANES, LANES), LANES)
            spectrum[group * upper:(group + 1) * upper, columns] = real.astype(jnp.bfloat16)
            spectrum[half_rows + group * upper:half_rows + (group + 1) * upper, columns] = (
                imag.astype(jnp.bfloat16)
            )

    depth = spectrum.shape[1]
    count = index_ref.shape[1]
    width = 256
    part = 256
    local = lax.broadcasted_iota(jnp.int32, (part, width), 0).astype(jnp.float32).astype(jnp.bfloat16)
    row_of = lax.broadcasted_iota(jnp.int32, (half_rows, width), 0)
    one = jnp.ones((part, width), jnp.bfloat16)
    zero = jnp.zeros((part, width), jnp.bfloat16)

    lines_per_step = width // LANES
    steps_per_block = chunk_lines // lines_per_step

    def select(phase, step):
        line = (step // steps_per_block) * tall + phase * chunk_lines
        line = line + (step % steps_per_block) * lines_per_step
        start = pl.multiple_of(line * LANES, width)
        index = index_ref[:, pl.ds(start, width)]
        column = index % depth
        upper_part = index // depth
        row = (upper_part % groups) * upper + upper_part // groups
        total = jnp.zeros((2 * half_rows, width), jnp.float32)
        for at in range(depth // part):
            shifted = (column - at * part).astype(jnp.float32).astype(jnp.bfloat16)
            chosen = jnp.where(local == jnp.broadcast_to(shifted, local.shape), one, zero)
            total = total + dot(spectrum[:, at * part:(at + 1) * part], chosen)
        mask = row_of == row
        real = jnp.sum(jnp.where(mask, total[:half_rows], 0.0), axis=0, keepdims=True)
        imag = jnp.sum(jnp.where(mask, total[half_rows:], 0.0), axis=0, keepdims=True)
        for side in range(lines_per_step):
            lanes = slice(side * LANES, (side + 1) * LANES)
            picked[pl.ds(line + side, 1), :] = real[:, lanes]
            picked[pl.ds(count // LANES + line + side, 1), :] = imag[:, lanes]

    def forward(phase):
        def one(i):
            source = behind(i)
            row_copy(phase, i, source).wait_recv()
            held = row_panel.at[source, c, lines_of(phase)]
            each(cols, lambda k: share(phase, i, k, held, c).start())

        each(rows, one)

    for phase in range(phases):

        @pl.loop(0, rows // 2 * steps_per_block, unroll=8)
        def _(step):
            select(phase, step)

        for block in range(rows):
            first = block * tall + phase * chunk_lines
            values = picked[first:first + chunk_lines, :].astype(jnp.bfloat16)
            by_row[block, phase * chunk_lines:(phase + 1) * chunk_lines, :] = values
            for at in range(chunk_lines // short):
                by_col[first // short + at] = picked[
                    first + at * short:first + (at + 1) * short, :
                ].astype(jnp.bfloat16)
        if phase == 0:
            pl.semaphore_wait(barrier, rows + cols - 2)
        each(rows, lambda i: row_copy(phase, i, r).start())

        def send_col(k):
            @pl.when(lax.rem(onward(k) * short // chunk_lines, phases) == phase)
            def _():
                col_copy(k, c).start()

        each(cols, send_col)
        held = by_row.at[r, lines_of(phase)]
        each(cols, lambda k: share(phase, 0, k, held, c).start())
        if phase > 0:
            forward(phase - 1)

    row_panel[r, c] = by_row[r]
    col_panel[r, c] = by_col[c]
    each(cols, lambda k: col_copy(k, back(k)).wait_recv())
    each(rows, lambda i: hand_on(i, r).start())
    forward(phases - 1)

    gap = lookup(conduction_band[...], conduction_energy[...]) - lookup(
        valence_band[...], valence_energy[...]
    )
    root = math.sqrt(gap.shape[0])
    for freq in range(weights.shape[1]):
        omega = imag_freq[:, freq:freq + 1]
        weights[:, freq:freq + 1] = -4.0 * gap / (gap * gap + omega * omega) / root

    each(cols, lambda k: col_copy(k, c).wait_send())

    def passed(i):
        hand_on(i, behind(i)).wait_recv()
        hand_on(i, r).wait_send()

    each(rows, passed)
    for phase in range(phases):
        each(rows, lambda i: row_copy(phase, i, r).wait_send())

        def finish(i, carry):
            held = row_panel.at[behind(i), c, lines_of(phase)]

            def ending(k):
                share(phase, i, k, held, back(k)).wait_recv()
                share(phase, i, k, held, c).wait_send()

            each(cols, ending)
            return carry

        lax.fori_loop(0, rows, finish, 0)


def transform(product, pw_index, row_count, col_count, *bands):
    bands = [values.reshape(1, -1) for values in bands]
    points = product.shape[0]
    count = pw_index.shape[0]
    lines = 2 * count // LANES
    tall, short = lines // row_count, lines // col_count
    phases = 2 if tall % 32 == 0 and (tall // 2) % short == 0 else 1
    tables = [jnp.asarray(table) for table in fourier_tables(points)]
    depth = 1024
    whole = pl.BlockSpec(memory_space=pltpu.VMEM)
    dma = pltpu.SemaphoreType.DMA
    return pl.pallas_call(
        transform_kernel,
        out_shape=(
            jax.ShapeDtypeStruct((row_count, col_count, tall, LANES), jnp.bfloat16),
            jax.ShapeDtypeStruct((row_count, col_count, short, LANES), jnp.bfloat16),
            jax.ShapeDtypeStruct((bands[0].shape[1], bands[-1].shape[1]), jnp.float32),
        ),
        in_specs=[whole] * (2 + len(tables) + len(bands)),
        out_specs=(whole, whole, whole),
        scratch_shapes=[
            pltpu.VMEM((points * points, 2 * points), jnp.float32),
            pltpu.VMEM((points**3 // depth, depth), jnp.bfloat16),
            pltpu.VMEM((lines, LANES), jnp.float32),
            pltpu.VMEM((row_count, tall, LANES), jnp.bfloat16),
            pltpu.VMEM((col_count, short, LANES), jnp.bfloat16),
            dma((phases, row_count)), dma((phases, row_count)),
            dma((col_count,)), dma((col_count,)),
            dma((phases, row_count, col_count)), dma((phases, row_count, col_count)),
            dma((row_count,)), dma((row_count,)),
        ],
        compiler_params=pltpu.CompilerParams(collective_id=0, has_side_effects=True),
        name="spectrum",
    )(product, pw_index.reshape(1, count), *tables, *bands)


def product_kernel(row_ref, col_ref, weight_ref, out_ref, row_lines, col_lines, left, right, ring, sems):
    pairs = row_ref.shape[0]
    freq_count, row_width, _ = out_ref.shape
    slots, height = ring.shape[0], ring.shape[1]

    for ref, lines, is_left in ((row_ref, row_lines, True), (col_ref, col_lines, False)):
        if len(ref.shape) == 3:
            blocks = ref.shape[1]
            lines[...] = ref[...].astype(jnp.float32).reshape(lines.shape)
        else:
            blocks = ref.shape[1] // LANES
        for block in range(blocks):
            lanes = slice(block * LANES, (block + 1) * LANES)
            if len(ref.shape) == 3:
                values = lines[pl.ds(block, pairs, stride=blocks), :]
            else:
                values = ref[:, lanes].astype(jnp.float32)
            if is_left:
                left[lanes, :] = values.T.astype(jnp.bfloat16)
            else:
                for freq in range(freq_count):
                    right[freq, :, lanes] = (
                        values * weight_ref[:, freq:freq + 1]
                    ).astype(jnp.bfloat16)

    steps = row_width // height

    def write(slot, freq, step):
        rows = pl.ds(pl.multiple_of(step * height, height), height)
        return pltpu.make_async_copy(ring.at[slot], out_ref.at[freq, rows], sems.at[slot])

    @pl.loop(0, steps)
    def _(step):
        panel = left[pl.ds(pl.multiple_of(step * height, height), height), :]
        for freq in range(freq_count):
            unit = step * freq_count + freq
            slot = lax.rem(unit, slots)

            @pl.when(unit >= slots)
            def _():
                write(slot, freq, step).wait()

            ring[slot] = dot(panel, right[freq])
            write(slot, freq, step).start()

    for slot in range(min(slots, steps * freq_count)):
        write(slot, 0, 0).wait()


def product(row_panel, col_panel, weights):
    pairs, freq_count = weights.shape
    row_width = row_panel.shape[2] * LANES
    col_width = col_panel.shape[2] * LANES
    panels = []
    lines = []
    for panel in (row_panel, col_panel):
        height = panel.shape[2]
        if height % 16 == 0:
            panels.append(panel.reshape(pairs, height, LANES))
            lines.append(pltpu.VMEM((pairs * height, LANES), jnp.float32))
        else:
            panels.append(panel.reshape(pairs, height * LANES))
            lines.append(pltpu.VMEM((8, LANES), jnp.float32))
    block = min(256, row_width)
    slots = 4
    whole = pl.BlockSpec(memory_space=pltpu.VMEM)
    return pl.pallas_call(
        product_kernel,
        out_shape=jax.ShapeDtypeStruct((freq_count, row_width, col_width), jnp.float32),
        in_specs=[whole, whole, whole],
        out_specs=pl.BlockSpec(memory_space=pl.ANY),
        scratch_shapes=lines + [
            pltpu.VMEM((row_width, pairs), jnp.bfloat16),
            pltpu.VMEM((freq_count, pairs, col_width), jnp.bfloat16),
            pltpu.VMEM((slots, block, col_width), jnp.float32),
            pltpu.SemaphoreType.DMA((slots,)),
        ],
        name="product",
    )(*panels, weights)


def shards(
    pair_products,
    pw_index,
    valence_band,
    conduction_band,
    valence_energy,
    conduction_energy,
    imag_freq,
):
    rows, cols = lax.axis_size("row"), lax.axis_size("col")
    row_panel, col_panel, weights = transform(
        pair_products[0], pw_index, rows, cols,
        valence_band, conduction_band, valence_energy, conduction_energy, imag_freq,
    )
    return product(row_panel, col_panel, weights)


def solution(mesh):
    in_specs = (P(("row", "col"), None, None, None), P(), P(), P(), P(), P(), P())
    out_specs = P(None, "row", "col")
    return jax.shard_map(shards, mesh=mesh, in_specs=in_specs, out_specs=out_specs, check_vma=False)
```

```python
import math

import jax
import jax.numpy as jnp
import numpy as np
from jax import lax
from jax.experimental import pallas as pl
from jax.experimental.pallas import tpu as pltpu
from jax.sharding import PartitionSpec as P

MESH = pl.DeviceIdType.MESH
LANES = 128


def split(values):
    high = values.astype(jnp.bfloat16)
    low = (values - high.astype(jnp.float32)).astype(jnp.bfloat16)
    return high, low


def fourier_tables(points):
    counter = np.arange(points)
    angles = (counter[:, None] * counter[None, :] % points) * (2.0 * math.pi / points)
    cosine, sine = np.cos(angles), np.sin(angles)
    upper = points // 2

    def halves(table):
        single = table.astype(np.float32)
        high = single.astype(jnp.bfloat16)
        return high, (single - high.astype(np.float32)).astype(jnp.bfloat16)

    along_z = np.concatenate(halves(np.concatenate([cosine, -sine], axis=1)), axis=0)
    high, low = halves(np.concatenate([cosine, sine], axis=0))
    along_y = np.concatenate([high, high, low], axis=1)
    scale = float(points) ** (-1.5)
    high, low = halves(np.concatenate([cosine[:upper], sine[:upper]], axis=0) * scale)
    along_x = np.concatenate([high, high, low], axis=1)
    return [along_z, along_y, along_x]


def dot(left, right):
    return lax.dot_general(
        left, right, (((1,), (0,)), ((), ())), preferred_element_type=jnp.float32
    )


def column_of(row):
    size = row.shape[1]
    here = lax.broadcasted_iota(jnp.int32, (size, size), 0)
    there = lax.broadcasted_iota(jnp.int32, (size, size), 1)
    return jnp.sum(jnp.where(here == there, row, 0.0), axis=1, keepdims=True)


def lookup(indices, table):
    column = column_of(indices.astype(jnp.float32))
    slots = lax.broadcasted_iota(jnp.int32, (column.shape[0], table.shape[1]), 1)
    return jnp.sum(
        jnp.where(column == slots.astype(jnp.float32), table, 0.0), axis=1, keepdims=True
    )


def transform_kernel(
    x_ref, index_ref, z_ref, y_ref, x_table_ref,
    valence_band, conduction_band, valence_energy, conduction_energy, imag_freq,
    row_panel, col_panel, weights,
    planes, spectrum, picked, by_row, by_col,
    row_send, row_recv, col_send, col_recv,
    share_send, share_recv, pass_send, pass_recv,
):
    rows, cols, tall = row_panel.shape[:3]
    short = col_panel.shape[2]
    phases = row_send.shape[0]
    chunk_lines = tall // phases
    r, c = lax.axis_index("row"), lax.axis_index("col")

    def each(count, action):
        def body(step, carry):
            action(step)
            return carry

        lax.fori_loop(1, count, body, 0)

    def ahead(i):
        return lax.rem(r + i, rows)

    def behind(i):
        return lax.rem(r - i + rows, rows)

    def onward(k):
        return lax.rem(c + k, cols)

    def back(k):
        return lax.rem(c - k + cols, cols)

    def remote(source, target, send, recv, device):
        return pltpu.make_async_remote_copy(
            src_ref=source, dst_ref=target, send_sem=send, recv_sem=recv,
            device_id=device, device_id_type=MESH)

    def lines_of(phase):
        return pl.ds(phase * chunk_lines, chunk_lines)

    def row_copy(phase, i, source):
        return remote(
            by_row.at[ahead(i), lines_of(phase)], row_panel.at[source, c, lines_of(phase)],
            row_send.at[phase, i], row_recv.at[phase, i], (ahead(i), c))

    def col_copy(k, source):
        return remote(
            by_col.at[onward(k)], col_panel.at[r, source],
            col_send.at[k], col_recv.at[k], (r, onward(k)))

    def share(phase, i, k, held, source):
        return remote(
            held, row_panel.at[behind(i), source, lines_of(phase)],
            share_send.at[phase, i, k], share_recv.at[phase, i, k], (r, onward(k)))

    def hand_on(i, source):
        return remote(
            col_panel.at[r], col_panel.at[source],
            pass_send.at[i], pass_recv.at[i], (ahead(i), c))

    barrier = pltpu.get_barrier_semaphore()
    each(rows, lambda i: pl.semaphore_signal(
        barrier, inc=1, device_id=(ahead(i), c), device_id_type=MESH))
    each(cols, lambda k: pl.semaphore_signal(
        barrier, inc=1, device_id=(r, onward(k)), device_id_type=MESH))

    points = x_ref.shape[0]
    upper = points // 2
    wide = 2 * points
    step = 8
    along_z, along_y, along_x = z_ref[...], y_ref[...], x_table_ref[...]
    sign = jnp.where(lax.broadcasted_iota(jnp.int32, (points, wide), 1) < points, 1.0, -1.0)

    @pl.loop(0, points // step, unroll=2)
    def _(block):
        start = pl.multiple_of(block * step, step)
        data = x_ref[pl.ds(start, step)].reshape(step * points, points)
        lines = dot(jnp.concatenate([data, data], axis=1), along_z)
        high, low = split(lines)
        for pair in range(step // 2):
            blocks = []
            for side in range(2):
                rows = slice((2 * pair + side) * points, (2 * pair + side + 1) * points)
                blocks.append(jnp.concatenate([high[rows], low[rows], high[rows]], axis=0))
            result = dot(along_y, jnp.concatenate(blocks, axis=1))
            for side in range(2):
                part = result[:, side * wide:(side + 1) * wide]
                rows = pl.ds(pl.multiple_of((start + 2 * pair + side) * points, points), points)
                planes[rows, :] = part[:points] + sign * pltpu.roll(part[points:], points, 1)

    per_group = spectrum.shape[1] // LANES
    groups = points // 2 // per_group
    half_rows = groups * upper
    first_half = lax.broadcasted_iota(jnp.int32, (upper, wide), 1) < points

    for group in range(groups):

        @pl.loop(0, per_group, unroll=8)
        def _(place):
            base = 2 * (group * per_group + place)
            blocks = []
            for side in range(2):
                high, low = split(planes[pl.ds(base + side, points, stride=points), :])
                blocks.append(jnp.concatenate([high, low, high], axis=0))
            result = dot(along_x, jnp.concatenate(blocks, axis=1))
            even_cos, odd_cos = result[:upper, :wide], result[:upper, wide:]
            even_sin, odd_sin = result[upper:, :wide], result[upper:, wide:]

            def join(left, right, turn_left, turn_right):
                left = pltpu.roll(left, points, 1) if turn_left else left
                right = pltpu.roll(right, points, 1) if turn_right else right
                return jnp.where(first_half, left, right)

            real = join(even_cos, odd_cos, False, True) + join(even_sin, odd_sin, True, False)
            imag = join(even_sin, odd_sin, False, True) - join(even_cos, odd_cos, True, False)
            columns = pl.ds(pl.multiple_of(place * LANES, LANES), LANES)
            spectrum[group * upper:(group + 1) * upper, columns] = real.astype(jnp.bfloat16)
            spectrum[half_rows + group * upper:half_rows + (group + 1) * upper, columns] = (
                imag.astype(jnp.bfloat16)
            )

    depth = spectrum.shape[1]
    count = index_ref.shape[1]
    width = 256
    part = 256
    local = lax.broadcasted_iota(jnp.int32, (part, width), 0).astype(jnp.float32).astype(jnp.bfloat16)
    row_of = lax.broadcasted_iota(jnp.int32, (half_rows, width), 0)
    one = jnp.ones((part, width), jnp.bfloat16)
    zero = jnp.zeros((part, width), jnp.bfloat16)

    lines_per_step = width // LANES
    steps_per_block = chunk_lines // lines_per_step

    def select(phase, step):
        line = (step // steps_per_block) * tall + phase * chunk_lines
        line = line + (step % steps_per_block) * lines_per_step
        start = pl.multiple_of(line * LANES, width)
        index = index_ref[:, pl.ds(start, width)]
        column = index % depth
        upper_part = index // depth
        row = (upper_part % groups) * upper + upper_part // groups
        total = jnp.zeros((2 * half_rows, width), jnp.float32)
        for at in range(depth // part):
            shifted = (column - at * part).astype(jnp.float32).astype(jnp.bfloat16)
            chosen = jnp.where(local == jnp.broadcast_to(shifted, local.shape), one, zero)
            total = total + dot(spectrum[:, at * part:(at + 1) * part], chosen)
        mask = row_of == row
        real = jnp.sum(jnp.where(mask, total[:half_rows], 0.0), axis=0, keepdims=True)
        imag = jnp.sum(jnp.where(mask, total[half_rows:], 0.0), axis=0, keepdims=True)
        for side in range(lines_per_step):
            lanes = slice(side * LANES, (side + 1) * LANES)
            picked[pl.ds(line + side, 1), :] = real[:, lanes]
            picked[pl.ds(count // LANES + line + side, 1), :] = imag[:, lanes]

    def forward(phase):
        def one(i):
            source = behind(i)
            row_copy(phase, i, source).wait_recv()
            held = row_panel.at[source, c, lines_of(phase)]
            each(cols, lambda k: share(phase, i, k, held, c).start())

        each(rows, one)

    def phase_of(block):
        return lax.rem(block * short // chunk_lines, phases)

    def pass_columns():
        col_panel[r, c] = by_col[c]
        each(cols, lambda k: col_copy(k, back(k)).wait_recv())
        each(rows, lambda i: hand_on(i, r).start())

    for phase in range(phases):

        @pl.loop(0, rows // 2 * steps_per_block, unroll=8)
        def _(step):
            select(phase, step)

        for block in range(rows):
            first = block * tall + phase * chunk_lines
            values = picked[first:first + chunk_lines, :].astype(jnp.bfloat16)
            by_row[block, phase * chunk_lines:(phase + 1) * chunk_lines, :] = values
            for at in range(chunk_lines // short):
                by_col[first // short + at] = picked[
                    first + at * short:first + (at + 1) * short, :
                ].astype(jnp.bfloat16)
        if phase == 0:
            pl.semaphore_wait(barrier, rows + cols - 2)
        each(rows, lambda i: row_copy(phase, i, r).start())

        def send_col(k):
            @pl.when(phase_of(onward(k)) == phase)
            def _():
                col_copy(k, c).start()

        each(cols, send_col)
        if phase > 0:
            pl.when(phase_of(c) == phase - 1)(pass_columns)
        held = by_row.at[r, lines_of(phase)]
        each(cols, lambda k: share(phase, 0, k, held, c).start())
        if phase > 0:
            forward(phase - 1)

    row_panel[r, c] = by_row[r]
    pl.when(phase_of(c) == phases - 1)(pass_columns)
    forward(phases - 1)

    gap = lookup(conduction_band[...], conduction_energy[...]) - lookup(
        valence_band[...], valence_energy[...]
    )
    root = math.sqrt(gap.shape[0])
    for freq in range(weights.shape[1]):
        omega = imag_freq[:, freq:freq + 1]
        weights[:, freq:freq + 1] = -4.0 * gap / (gap * gap + omega * omega) / root

    each(cols, lambda k: col_copy(k, c).wait_send())

    def passed(i):
        hand_on(i, behind(i)).wait_recv()
        hand_on(i, r).wait_send()

    each(rows, passed)
    for phase in range(phases):
        each(rows, lambda i: row_copy(phase, i, r).wait_send())

        def finish(i, carry):
            held = row_panel.at[behind(i), c, lines_of(phase)]

            def ending(k):
                share(phase, i, k, held, back(k)).wait_recv()
                share(phase, i, k, held, c).wait_send()

            each(cols, ending)
            return carry

        lax.fori_loop(0, rows, finish, 0)


def transform(product, pw_index, row_count, col_count, *bands):
    bands = [values.reshape(1, -1) for values in bands]
    points = product.shape[0]
    count = pw_index.shape[0]
    lines = 2 * count // LANES
    tall, short = lines // row_count, lines // col_count
    phases = 2 if tall % 32 == 0 and (tall // 2) % short == 0 else 1
    tables = [jnp.asarray(table) for table in fourier_tables(points)]
    depth = 1024
    whole = pl.BlockSpec(memory_space=pltpu.VMEM)
    dma = pltpu.SemaphoreType.DMA
    return pl.pallas_call(
        transform_kernel,
        out_shape=(
            jax.ShapeDtypeStruct((row_count, col_count, tall, LANES), jnp.bfloat16),
            jax.ShapeDtypeStruct((row_count, col_count, short, LANES), jnp.bfloat16),
            jax.ShapeDtypeStruct((bands[0].shape[1], bands[-1].shape[1]), jnp.float32),
        ),
        in_specs=[whole] * (2 + len(tables) + len(bands)),
        out_specs=(whole, whole, whole),
        scratch_shapes=[
            pltpu.VMEM((points * points, 2 * points), jnp.float32),
            pltpu.VMEM((points**3 // depth, depth), jnp.bfloat16),
            pltpu.VMEM((lines, LANES), jnp.float32),
            pltpu.VMEM((row_count, tall, LANES), jnp.bfloat16),
            pltpu.VMEM((col_count, short, LANES), jnp.bfloat16),
            dma((phases, row_count)), dma((phases, row_count)),
            dma((col_count,)), dma((col_count,)),
            dma((phases, row_count, col_count)), dma((phases, row_count, col_count)),
            dma((row_count,)), dma((row_count,)),
        ],
        compiler_params=pltpu.CompilerParams(collective_id=0, has_side_effects=True),
        name="spectrum",
    )(product, pw_index.reshape(1, count), *tables, *bands)


def product_kernel(row_ref, col_ref, weight_ref, out_ref, row_lines, col_lines, left, right, ring, sems):
    pairs = row_ref.shape[0]
    freq_count, row_width, _ = out_ref.shape
    slots, height = ring.shape[0], ring.shape[1]

    for ref, lines, is_left in ((row_ref, row_lines, True), (col_ref, col_lines, False)):
        if len(ref.shape) == 3:
            blocks = ref.shape[1]
            lines[...] = ref[...].astype(jnp.float32).reshape(lines.shape)
        else:
            blocks = ref.shape[1] // LANES
        for block in range(0 if is_left else blocks):
            lanes = slice(block * LANES, (block + 1) * LANES)
            if len(ref.shape) == 3:
                values = lines[pl.ds(block, pairs, stride=blocks), :]
            else:
                values = ref[:, lanes].astype(jnp.float32)
            if not is_left:
                for freq in range(freq_count):
                    right[freq, :, lanes] = (
                        values * weight_ref[:, freq:freq + 1]
                    ).astype(jnp.bfloat16)

    steps = row_width // height

    def write(slot, freq, step):
        rows = pl.ds(pl.multiple_of(step * height, height), height)
        return pltpu.make_async_copy(ring.at[slot], out_ref.at[freq, rows], sems.at[slot])

    @pl.loop(0, steps)
    def _(step):
        for part in range(height // LANES):
            block = step * (height // LANES) + part
            if len(row_ref.shape) == 3:
                values = row_lines[pl.ds(block, pairs, stride=row_ref.shape[1]), :]
            else:
                values = row_ref[:, pl.ds(pl.multiple_of(block * LANES, LANES), LANES)]
                values = values.astype(jnp.float32)
            left[part * LANES:(part + 1) * LANES, :] = values.T.astype(jnp.bfloat16)
        panel = left[...]
        for freq in range(freq_count):
            unit = step * freq_count + freq
            slot = lax.rem(unit, slots)

            @pl.when(unit >= slots)
            def _():
                write(slot, freq, step).wait()

            ring[slot] = dot(panel, right[freq])
            write(slot, freq, step).start()

    for slot in range(min(slots, steps * freq_count)):
        write(slot, 0, 0).wait()


def product(row_panel, col_panel, weights):
    pairs, freq_count = weights.shape
    row_width = row_panel.shape[2] * LANES
    col_width = col_panel.shape[2] * LANES
    panels = []
    lines = []
    for panel in (row_panel, col_panel):
        height = panel.shape[2]
        if height % 16 == 0:
            panels.append(panel.reshape(pairs, height, LANES))
            lines.append(pltpu.VMEM((pairs * height, LANES), jnp.float32))
        else:
            panels.append(panel.reshape(pairs, height * LANES))
            lines.append(pltpu.VMEM((8, LANES), jnp.float32))
    block = min(256, row_width)
    slots = 4
    whole = pl.BlockSpec(memory_space=pltpu.VMEM)
    return pl.pallas_call(
        product_kernel,
        out_shape=jax.ShapeDtypeStruct((freq_count, row_width, col_width), jnp.float32),
        in_specs=[whole, whole, whole],
        out_specs=pl.BlockSpec(memory_space=pl.ANY),
        scratch_shapes=lines + [
            pltpu.VMEM((block, pairs), jnp.bfloat16),
            pltpu.VMEM((freq_count, pairs, col_width), jnp.bfloat16),
            pltpu.VMEM((slots, block, col_width), jnp.float32),
            pltpu.SemaphoreType.DMA((slots,)),
        ],
        name="product",
    )(*panels, weights)


def shards(
    pair_products,
    pw_index,
    valence_band,
    conduction_band,
    valence_energy,
    conduction_energy,
    imag_freq,
):
    rows, cols = lax.axis_size("row"), lax.axis_size("col")
    row_panel, col_panel, weights = transform(
        pair_products[0], pw_index, rows, cols,
        valence_band, conduction_band, valence_energy, conduction_energy, imag_freq,
    )
    return product(row_panel, col_panel, weights)


def solution(mesh):
    in_specs = (P(("row", "col"), None, None, None), P(), P(), P(), P(), P(), P())
    out_specs = P(None, "row", "col")
    return jax.shard_map(shards, mesh=mesh, in_specs=in_specs, out_specs=out_specs, check_vma=False)
```
